512 devices in a mesh: depth: 16 (over y, core), lat: 32 (over x, z).
Axes of the slice: x: 4, y: 8, z: 8, core: 2. Of those that a mesh axis runs over, the one named last changes fastest.
Arguments:
- slices: float32 [48, 2, 256, 8192], P('depth', None, None, 'lat'), may hold values from -1.23 to 1.23, as said below
- section_counts: int32 [16], P('depth'), may hold values from 1 to 3, as said below
- scan_rows: int32 [256], P('lat'), may hold values from 0 to 128, as said below
- scan_columns: int32 [256], P('lat'), may hold values from 0 to 256, as said below
- tick_order: int32 [32, 8], P('lat'), may hold values from 0 to 7, each once within a row
- measured: float32 [256, 128, 128], P('lat'), may hold values from 0.2 to 2
- illumination: float32 [2, 128, 128], replicated, may hold values from -4.2 to 4.2
Outputs:
- slice_grad: float32 [48, 2, 256, 8192], P('depth', None, None, 'lat')
- position_loss: float32 [32, 8], P('lat')
The draws below stay inside these ranges and needn't reach their ends.
Inputs may be any that keep to these rules, and one draw needn't show every extreme that they name: `slices`: the real and imaginary parts of transmission values of magnitude near one. `section_counts`: some section uses all 3 slots and some other section uses one. `scan_rows`: both ends are reached in every draw. `scan_columns`: a window may reach up to 128 columns into the next tile, the last tile continuing into the first; both ends are reached in every draw. `tick_order`: each row lists the tile's 8 positions once.
All inputs are finite; a program needn't handle non-finite values.
Results may differ from the reference program's by a relative error of at most 0.0003.
Values sent between devices are 32-bit elements; how exact they have to be, the bound alone decides.
No kernel may reach another device: no remote copies, remote signals or barrier semaphores. Data moves between devices by JAX's collectives and lax.ppermute only.
A program may use at most 128 MiB of HBM per device.

```python
import math
import jax
import jax.numpy as jnp
from jax import lax

W = 128
TILE = 256
MAXS = 3
POS = 8
SLOTS = 48
POSITIONS = 256
N_DEPTH = 16
N_LAT = 32


def draw_slices(key, part):
    first, second = jax.random.split(key)
    shape = (SLOTS, TILE, TILE * N_LAT)
    amplitude = jnp.exp(jax.random.uniform(first, shape, jnp.float32, -0.2, 0.2))
    phase = jax.random.uniform(second, shape, jnp.float32, -jnp.pi, jnp.pi)
    return jnp.stack([amplitude * jnp.cos(phase), amplitude * jnp.sin(phase)], axis=1)


def draw_section_counts(key, part):
    first, second, third = jax.random.split(jax.random.fold_in(key, 11), 3)
    values = jax.random.randint(first, (N_DEPTH,), 1, MAXS + 1)
    place = jax.random.randint(second, (), 0, N_DEPTH)
    other = (place + 1 + jax.random.randint(third, (), 0, N_DEPTH - 1)) % N_DEPTH
    return values.at[other].set(1).at[place].set(MAXS)


def ends_draw(key, top):
    first, second, third = jax.random.split(key, 3)
    values = jax.random.randint(first, (POS * N_LAT,), 0, top + 1)
    place = jax.random.randint(second, (), 0, POS * N_LAT)
    other = (place + 1 + jax.random.randint(third, (), 0, POS * N_LAT - 1)) % (POS * N_LAT)
    return values.at[other].set(0).at[place].set(top)


def draw_scan_rows(key, part):
    return ends_draw(jax.random.fold_in(key, 23), TILE - W)


def draw_scan_columns(key, part):
    return ends_draw(jax.random.fold_in(key, 37), TILE)


def levels(stream_key, dims, cuts, low, largest):
    level, own = 1.0, jax.random.fold_in(stream_key, 6)
    for axis_at, shards_of in cuts:
        steps = jnp.exp(jax.random.uniform(jax.random.fold_in(own, axis_at), (shards_of,), jnp.float32, low / len(cuts), largest / len(cuts)))
        level = level * jnp.repeat(steps, dims[axis_at] // shards_of).reshape([-1 if axis == axis_at else 1 for axis in range(len(dims))])
    return level


def scatter_about(key, dims, scale, limit, kind=jnp.bfloat16):
    return jnp.clip(scale * jax.random.normal(key, dims, jnp.float32), -limit, limit).astype(kind)


def setup_inputs(seed: int = 0) -> dict:
    key_list = jax.random.split(jax.random.key(seed), 8)
    return {
        "slices": draw_slices(jax.random.fold_in(key_list[7], 71), 0),
        "section_counts": draw_section_counts(jax.random.fold_in(key_list[7], 71), 0),
        "scan_rows": draw_scan_rows(jax.random.fold_in(key_list[7], 71), 0),
        "scan_columns": draw_scan_columns(jax.random.fold_in(key_list[7], 71), 0),
        "tick_order": jax.vmap(lambda own: jax.random.permutation(own, POS))(jax.random.split(key_list[4], N_LAT)).reshape((N_LAT, POS)).astype(jnp.int32),
        "measured": jnp.clip(0.2 + 1.8 * jax.random.uniform(key_list[5], (POSITIONS, W, W), jnp.float32) ** levels(key_list[5], (POSITIONS, W, W), ((0, 32),), -0.2, 0.2), 0.2, 2.0),
        "illumination": scatter_about(key_list[6], (2, W, W), 0.7, 4.2, jnp.float32),
    }


fresnel = 12.0
highest = lax.Precision.HIGHEST

def dft_blocks(width, sign):
    index = jnp.arange(width, dtype=jnp.int32)
    product = index[:, None] * index[None, :] % width
    angle = 2.0 * math.pi / width * product.astype(jnp.float32)
    scale = 1.0 / math.sqrt(width)
    cosine = jnp.cos(angle) * scale
    sine = sign * jnp.sin(angle) * scale
    return jnp.stack([jnp.stack([cosine, sine]), jnp.stack([-sine, cosine])])

def make_tables(width):
    index = jnp.arange(width, dtype=jnp.int32)
    frequency = ((index + width // 2) % width - width // 2).astype(jnp.float32) / width
    phase = -fresnel * (frequency[:, None] * frequency[:, None] + frequency[None, :] * frequency[None, :])
    return (dft_blocks(width, -1.0), dft_blocks(width, 1.0), jnp.cos(phase), jnp.sin(phase))

def transform(fields, blocks):
    half = jnp.einsum('bcyx,cdxk->bdyk', fields, blocks, precision=highest)
    return jnp.einsum('cdky,bcyx->bdkx', blocks, half, precision=highest)

def complex_product(first, second, conjugate):
    sign = -1.0 if conjugate else 1.0
    first_real = first[:, 0]
    first_imag = sign * first[:, 1]
    real_part = first_real * second[:, 0] - first_imag * second[:, 1]
    imag_part = first_real * second[:, 1] + first_imag * second[:, 0]
    return jnp.stack([real_part, imag_part], axis=1)

def propagate(fields, tables, adjoint):
    forward_blocks, inverse_blocks, kernel_cos, kernel_sin = tables
    spectrum = transform(fields, forward_blocks)
    kernel_imag = -kernel_sin if adjoint else kernel_sin
    real_part = spectrum[:, 0] * kernel_cos - spectrum[:, 1] * kernel_imag
    imag_part = spectrum[:, 0] * kernel_imag + spectrum[:, 1] * kernel_cos
    return transform(jnp.stack([real_part, imag_part], axis=1), inverse_blocks)

def forward_loss(windows, active, start_wave, target, tables):

    def one_slice(fields, inputs):
        window, flag = inputs

        def advance(current):
            return propagate(complex_product(current, window[None], False), tables, False)

        def keep(current):
            return current
        return (lax.cond(flag, advance, keep, fields), None)
    fields, _ = lax.scan(one_slice, start_wave[None], (windows, active))
    spectrum = transform(fields, tables[0])
    misfit = spectrum[0, 0] * spectrum[0, 0] + spectrum[0, 1] * spectrum[0, 1] - target
    return (jnp.sum(misfit * misfit), jnp.mean(misfit * misfit))

def reference(slices, section_counts, scan_rows, scan_columns, tick_order, measured, illumination):
    width = illumination.shape[-1]
    tables = make_tables(width)
    slot_index = jnp.arange(MAXS, dtype=jnp.int32)
    active = (slot_index[None, :] < section_counts[:, None]).reshape(-1)
    zero = jnp.zeros((), jnp.int32)

    def one_tile(carry, tile):
        own = lax.dynamic_slice_in_dim(slices, (tile * TILE).astype(jnp.int32), TILE, 3)
        after = lax.dynamic_slice_in_dim(slices, ((tile + 1) % N_LAT * TILE).astype(jnp.int32), width, 3)
        extended = jnp.concatenate([own, after], axis=3)

        def one_position(gradient, local):
            index = tile * POS + local
            corner = (zero, zero, scan_rows[index].astype(jnp.int32), scan_columns[index].astype(jnp.int32))
            windows = lax.dynamic_slice(extended, corner, (SLOTS, 2, width, width))

            def loss_only(cut):
                return forward_loss(cut, active, illumination, measured[index], tables)
            total, pull, mean = jax.vjp(loss_only, windows, has_aux=True)
            pulled, = pull(jnp.ones_like(total))
            old = lax.dynamic_slice(gradient, corner, (SLOTS, 2, width, width))
            gradient = lax.dynamic_update_slice(gradient, old + pulled, corner)
            return (gradient, mean)
        start = jnp.zeros((SLOTS, 2, TILE, TILE + width), jnp.float32)
        gradient, means = lax.scan(one_position, start, jnp.arange(POS, dtype=jnp.int32))
        ordered = means[tick_order[tile]]
        return (carry, (gradient[..., :TILE], gradient[..., TILE:], ordered))
    _, (main, rims, ordered) = lax.scan(one_tile, jnp.zeros((), jnp.float32), jnp.arange(N_LAT, dtype=jnp.int32))
    main = main.at[..., :width].add(jnp.roll(rims, 1, axis=0))
    slice_grad = jnp.transpose(main, (1, 2, 3, 0, 4)).reshape(SLOTS, 2, TILE, N_LAT * TILE)
    return (slice_grad, ordered)
```

```python
import functools

import jax
import jax.numpy as jnp
import numpy as np
from jax import lax
from jax.experimental import pallas as pl
from jax.experimental.pallas import tpu as pltpu
from jax.sharding import PartitionSpec as P

FRESNEL = 12.0
W = 128
f32 = jnp.float32
bf16 = jnp.bfloat16


def moved(block, axis, distance):
    count = lax.axis_size(axis)
    return lax.ppermute(block, axis, [((i - distance) % count, i) for i in range(count)])


def swapped(block):
    count = lax.axis_size("depth")
    return lax.ppermute(block, "depth", [(i ^ 1, i) for i in range(count)])


def three_parts(array):
    parts = []
    rest = np.asarray(array, np.float64)
    for _ in range(3):
        part = rest.astype(np.float32).astype(bf16)
        parts.append(part)
        rest = rest - part.astype(np.float64)
    return parts


def right_table(matrix):
    first, second, third = three_parts(np.concatenate([matrix.real, matrix.imag], 1))
    return np.concatenate([first, first, second, third], 0)


def left_table(matrix):
    first, second, third = three_parts(np.concatenate([matrix.real, matrix.imag], 0))
    return np.concatenate(
        [np.concatenate([first, first], 1), np.concatenate([second, third], 1)], 0
    )


def make_tables(width):
    index = np.arange(width)
    fourier = np.exp(-2j * np.pi * (np.outer(index, index) % width) / width) / np.sqrt(width)
    frequency = ((index + width // 2) % width - width // 2) / width
    chirp = np.exp(-1j * FRESNEL * frequency * frequency)
    step = np.conj(fourier) @ (chirp[:, None] * fourier)
    return tuple(make(matrix) for matrix in (step, fourier) for make in (right_table, left_table))


def halves(value):
    high = value.astype(bf16)
    return high, (value - high.astype(f32)).astype(bf16)


def product(a, b):
    return jnp.dot(a, b, preferred_element_type=f32)


def two_sided(real, imag, right, left, conjugate):
    high, low = halves(jnp.concatenate([real, imag], 0))
    z = product(jnp.concatenate([high, low], 1), right[: 2 * W]) + product(
        jnp.concatenate([high, high], 1), right[2 * W :]
    )
    if conjugate:
        y = jnp.concatenate([z[:W, :W] + z[W:, W:], z[W:, :W] - z[:W, W:]], 1)
    else:
        y = jnp.concatenate([z[:W, :W] - z[W:, W:], z[:W, W:] + z[W:, :W]], 1)
    high, low = halves(y)
    z = product(left[: 2 * W], jnp.concatenate([high, low], 0)) + product(
        left[2 * W :], jnp.concatenate([high, high], 0)
    )
    if conjugate:
        return z[:W, :W] + z[W:, W:], z[:W, W:] - z[W:, :W]
    return z[:W, :W] - z[W:, W:], z[:W, W:] + z[W:, :W]


def cut_kernel(rows, columns, count, own, rim, out, extended):
    slots = own.shape[0]
    positions = out.shape[0]
    tile = own.shape[3]
    for slot in range(slots):
        for part in range(2):
            extended[2 * slot + part, :, :tile] = own[slot, part]
            extended[2 * slot + part, :, tile:] = rim[slot, part]
    lane = lax.broadcasted_iota(jnp.int32, (W + 8, W), 1)
    stamp = jnp.full((8, W), count[0], jnp.int32).astype(f32)

    def one_position(p, carry):
        row = pl.multiple_of(jnp.minimum(rows[p] // 8 * 8, tile - W - 8), 8)
        lift = (W + 8 - (rows[p] - row)) % (W + 8)
        block = jnp.minimum(columns[p] // W, tile // W - 1)
        shift = columns[p] - block * W
        turn = (W - shift) % W
        start = pl.multiple_of(block * W, W)
        after = pl.multiple_of(block * W + W, W)
        for plane in range(2 * slots):
            first = extended[plane, pl.ds(row, W + 8), pl.ds(start, W)]
            second = extended[plane, pl.ds(row, W + 8), pl.ds(after, W)]
            both = jnp.where(
                lane < W - shift, pltpu.roll(first, turn, 1), pltpu.roll(second, turn, 1)
            )
            out[p, plane * W : (plane + 1) * W, :] = pltpu.roll(both, lift, 0)[:W]
        out[p, 2 * slots * W :, :] = stamp
        return carry

    lax.fori_loop(0, positions, one_position, 0)


def two_sided_each(fields, right, left, conjugate):
    stacked = [halves(jnp.concatenate([real, imag], 0)) for real, imag in fields]
    first = jnp.concatenate([jnp.concatenate([high, low], 1) for high, low in stacked], 0)
    second = jnp.concatenate([jnp.concatenate([high, high], 1) for high, low in stacked], 0)
    every = product(first, right[: 2 * W]) + product(second, right[2 * W :])
    results = []
    for index in range(len(fields)):
        z = every[index * 2 * W : (index + 1) * 2 * W]
        if conjugate:
            y = jnp.concatenate([z[:W, :W] + z[W:, W:], z[W:, :W] - z[:W, W:]], 1)
        else:
            y = jnp.concatenate([z[:W, :W] - z[W:, W:], z[:W, W:] + z[W:, :W]], 1)
        high, low = halves(y)
        z = product(left[: 2 * W], jnp.concatenate([high, low], 0)) + product(
            left[2 * W :], jnp.concatenate([high, high], 0)
        )
        if conjugate:
            results.append((z[:W, :W] + z[W:, W:], z[:W, W:] - z[W:, :W]))
        else:
            results.append((z[:W, :W] - z[W:, W:], z[:W, W:] + z[W:, :W]))
    return results


def times(a, b):
    return a[0] * b[0] - a[1] * b[1], a[0] * b[1] + a[1] * b[0]


def times_conjugate(a, b):
    return a[0] * b[0] + a[1] * b[1], a[0] * b[1] - a[1] * b[0]


def wave_kernel(
    core_ref, mine, other, wanted, illumination, step_right, step_left, far_right, far_left, out, counts
):
    chips = mine.shape[0]
    planes = (mine.shape[1] - 8) // W
    sections = 2 * chips
    core = core_ref[0]
    for chip in range(chips):
        own = jnp.max(mine[chip, planes * W :, :]).astype(jnp.int32)
        its = jnp.max(other[chip, planes * W :, :]).astype(jnp.int32)
        counts[2 * chip] = jnp.where(core == 0, own, its)
        counts[2 * chip + 1] = jnp.where(core == 0, its, own)

    def window(section, slot):
        chip = section // 2
        local = section % 2 == core
        at = pl.multiple_of(slot * 2 * W, 2 * W)
        return tuple(
            jnp.where(
                local,
                mine[chip, pl.ds(at + part * W, W), :],
                other[chip, pl.ds(at + part * W, W), :],
            )
            for part in range(2)
        )

    def keep(chip, field):
        out[chip, :W, :] = field[0]
        out[chip, W : 2 * W, :] = field[1]

    def last_of(section):
        return counts[section] - (section == sections - 1).astype(jnp.int32)

    def forward_section(section, field):
        @pl.when((core == 0) & (section % 2 == 0))
        def _():
            keep(section // 2, field)

        def one(slot, value):
            value = times(value, window(section, slot))
            return two_sided(*value, step_right[...], step_left[...], False)

        return lax.fori_loop(0, last_of(section), one, field)

    def backward_section(index, field):
        section = sections - 1 - index

        @pl.when((section % 2 == 1) & (index > 0))
        def _():
            keep(section // 2, field)

        top = last_of(section)

        def one(step, value):
            spread = two_sided(*value, step_right[...], step_left[...], True)
            return times_conjugate(window(section, top - 1 - step), spread)

        return lax.fori_loop(0, jnp.where(section == 1, 0, top), one, field)

    field = lax.fori_loop(0, sections, forward_section, (illumination[0], illumination[1]))
    final = counts[sections - 1] - 1
    field = times(field, window(sections - 1, final))
    real, imag = two_sided(*field, far_right[...], far_left[...], False)
    misfit = real * real + imag * imag - wanted[...]
    loss = jnp.sum(misfit * misfit) * (1.0 / (W * W))
    for chip in range(chips):
        out[chip, 2 * W :, :] = jnp.full((8, W), loss, f32)

    @pl.when(core == 1)
    def _():
        spread = two_sided(
            4.0 * misfit * real, 4.0 * misfit * imag, far_right[...], far_left[...], True
        )
        keep(chips - 1, spread)
        start = times_conjugate(window(sections - 1, final), spread)
        lax.fori_loop(0, sections - 1, backward_section, start)


GROUP = 4


def fields_of(ref, group, at):
    return [
        tuple(ref[group * GROUP + each, pl.ds(at + part * W, W), :] for part in range(2))
        for each in range(GROUP)
    ]


def put_fields(ref, group, at, fields):
    for each in range(GROUP):
        for part in range(2):
            ref[group * GROUP + each, pl.ds(at + part * W, W), :] = fields[each][part]


def first_kernel(place, count, windows, arrived, step_right, step_left, track, handed):
    core = place[0] % 2
    top = count[0]
    groups = windows.shape[0] // GROUP

    @pl.when(core == 0)
    def _():
        def one_group(group, carry):
            put_fields(handed, group, 0, fields_of(arrived, group, 0))

            def one(slot, inner):
                at = pl.multiple_of(slot * 2 * W, 2 * W)
                fields = fields_of(handed, group, 0)
                put_fields(track, group, at, fields)
                cut = fields_of(windows, group, at)
                fields = [times(a, b) for a, b in zip(fields, cut)]
                put_fields(
                    handed, group, 0, two_sided_each(fields, step_right[...], step_left[...], False)
                )
                return inner

            return lax.fori_loop(0, top, one, carry)

        lax.fori_loop(0, groups, one_group, 0)

    @pl.when(core == 1)
    def _():
        def one_group(group, carry):
            put_fields(handed, group, 0, fields_of(arrived, group, 0))

            def one(step, inner):
                at = pl.multiple_of((top - 1 - step) * 2 * W, 2 * W)
                fields = fields_of(handed, group, 0)
                spread = two_sided_each(fields, step_right[...], step_left[...], True)
                done = (step == 0) & (place[0] == place[1] - 1)
                spread = [
                    tuple(jnp.where(done, kept, fresh) for kept, fresh in zip(a, b))
                    for a, b in zip(fields, spread)
                ]
                put_fields(track, group, at, spread)
                cut = fields_of(windows, group, at)
                put_fields(handed, group, 0, [times_conjugate(a, b) for a, b in zip(cut, spread)])
                return inner

            return lax.fori_loop(0, top, one, carry)

        lax.fori_loop(0, groups, one_group, 0)


def second_kernel(place, count, windows, track, handed, step_right, step_left, pulls, state):
    core = place[0] % 2
    top = count[0]
    groups = windows.shape[0] // GROUP

    @pl.when(core == 0)
    def _():
        def one_group(group, carry):
            put_fields(state, group, 0, fields_of(handed, group, 0))

            def one(step, inner):
                at = pl.multiple_of((top - 1 - step) * 2 * W, 2 * W)
                fields = fields_of(state, group, 0)
                spread = two_sided_each(fields, step_right[...], step_left[...], True)
                waves = fields_of(track, group, at)
                put_fields(pulls, group, at, [times_conjugate(a, b) for a, b in zip(waves, spread)])
                cut = fields_of(windows, group, at)
                put_fields(state, group, 0, [times_conjugate(a, b) for a, b in zip(cut, spread)])
                return inner

            return lax.fori_loop(0, top, one, carry)

        lax.fori_loop(0, groups, one_group, 0)

    @pl.when(core == 1)
    def _():
        def one_group(group, carry):
            put_fields(state, group, 0, fields_of(handed, group, 0))

            def pull(slot):
                at = pl.multiple_of(slot * 2 * W, 2 * W)
                fields = fields_of(state, group, 0)
                spread = fields_of(track, group, at)
                put_fields(pulls, group, at, [times_conjugate(a, b) for a, b in zip(fields, spread)])
                return fields, at

            def one(slot, inner):
                fields, at = pull(slot)
                cut = fields_of(windows, group, at)
                fields = [times(a, b) for a, b in zip(fields, cut)]
                put_fields(
                    state, group, 0, two_sided_each(fields, step_right[...], step_left[...], False)
                )
                return inner

            lax.fori_loop(0, top - 1, one, carry)
            pull(top - 1)
            return carry

        lax.fori_loop(0, groups, one_group, 0)


def deposit_kernel(rows, columns, count, order, pulls, arrived, main, rim, losses, total):
    positions = pulls.shape[0]
    planes = pulls.shape[1] // W
    tile = main.shape[3]
    total[...] = jnp.zeros_like(total)
    lane = lax.broadcasted_iota(jnp.int32, (W + 8, W), 1)
    spare = jnp.zeros((8, W), f32)

    def one_position(p, carry):
        row = pl.multiple_of(jnp.minimum(rows[p] // 8 * 8, tile - W - 8), 8)
        drop = rows[p] - row
        block = jnp.minimum(columns[p] // W, tile // W - 1)
        shift = columns[p] - block * W
        start = pl.multiple_of(block * W, W)
        after = pl.multiple_of(block * W + W, W)

        def one_slot(slot, inner):
            for part in range(2):
                at = pl.multiple_of((2 * slot + part) * W, W)
                pull = jnp.concatenate([pulls[p, pl.ds(at, W), :], spare], 0)
                pull = pltpu.roll(pltpu.roll(pull, drop, 0), shift % W, 1)
                plane = 2 * slot + part
                total[plane, pl.ds(row, W + 8), pl.ds(start, W)] += jnp.where(lane >= shift, pull, 0.0)
                total[plane, pl.ds(row, W + 8), pl.ds(after, W)] += jnp.where(lane < shift, pull, 0.0)
            return inner

        return lax.fori_loop(0, count[0], one_slot, carry)

    lax.fori_loop(0, positions, one_position, 0)
    for plane in range(planes):
        main[plane // 2, plane % 2] = total[plane, :, :tile]
        rim[plane // 2, plane % 2] = total[plane, :, tile:]
    place = lax.broadcasted_iota(jnp.int32, (1, W), 1)
    line = jnp.zeros((1, W), f32)
    for j in range(positions):
        line = jnp.where(place == j, arrived[order[0, j], 2 * W : 2 * W + 1, :], line)
    losses[...] = line[:, :positions]


def merge_kernel(main, rim, out):
    out[:, :, :, W:] = main[:, :, :, W:]
    out[:, :, :, :W] = main[:, :, :, :W] + rim[...]


VMEM = pl.BlockSpec(memory_space=pltpu.VMEM)
SMEM = pl.BlockSpec(memory_space=pltpu.SMEM)


def shards(slices, section_counts, scan_rows, scan_columns, tick_order, measured, illumination):
    slots = slices.shape[0]
    tile = slices.shape[3]
    positions = scan_rows.shape[0]
    planes = 2 * slots
    length = planes * W + 8
    chips = lax.axis_size("depth") // 2
    place = lax.axis_index("depth")
    groups = [[2 * chip + core for chip in range(chips)] for core in range(2)]
    exchange = functools.partial(
        lax.all_to_all, axis_name="depth", split_axis=0, concat_axis=0, tiled=True, axis_index_groups=groups
    )
    params = pltpu.CompilerParams(vmem_limit_bytes=48 << 20)
    tables = [jnp.asarray(table) for table in make_tables(W)]
    message = jax.ShapeDtypeStruct((positions, length, W), f32)

    rim = moved(slices[..., :W], "lat", -1)
    outgoing = pl.pallas_call(
        cut_kernel,
        out_shape=message,
        in_specs=[SMEM] * 3 + [VMEM] * 2,
        out_specs=VMEM,
        scratch_shapes=[pltpu.VMEM((planes, tile, tile + W), f32)],
        compiler_params=params,
        name="cut",
    )(scan_rows, scan_columns, section_counts, slices, rim)
    mine = exchange(outgoing)
    other = swapped(mine)
    wanted = lax.dynamic_index_in_dim(measured, place // 2, 0, keepdims=False)
    boundary = pl.pallas_call(
        wave_kernel,
        out_shape=jax.ShapeDtypeStruct((chips, 2 * W + 8, W), f32),
        in_specs=[SMEM] + [VMEM] * 8,
        out_specs=VMEM,
        scratch_shapes=[pltpu.SMEM((2 * chips,), jnp.int32)],
        compiler_params=params,
        name="wave",
    )((place % 2).reshape(1), mine, other, wanted, illumination, *tables)
    arrived = exchange(boundary)
    spot = jnp.stack([place, jnp.int32(2 * chips)])
    field = jax.ShapeDtypeStruct((positions, 2 * W, W), f32)
    stack = jax.ShapeDtypeStruct((positions, planes * W, W), f32)
    track, handed = pl.pallas_call(
        first_kernel,
        out_shape=(stack, field),
        in_specs=[SMEM] * 2 + [VMEM] * 4,
        out_specs=(VMEM,) * 2,
        compiler_params=params,
        name="first",
    )(spot, section_counts, outgoing, arrived, *tables[:2])
    pulls = pl.pallas_call(
        second_kernel,
        out_shape=stack,
        in_specs=[SMEM] * 2 + [VMEM] * 5,
        out_specs=VMEM,
        scratch_shapes=[pltpu.VMEM((positions, 2 * W, W), f32)],
        compiler_params=params,
        name="second",
    )(spot, section_counts, outgoing, track, swapped(handed), *tables[:2])
    main, overflow, losses = pl.pallas_call(
        deposit_kernel,
        out_shape=(
            jax.ShapeDtypeStruct((slots, 2, tile, tile), f32),
            jax.ShapeDtypeStruct((slots, 2, tile, W), f32),
            jax.ShapeDtypeStruct((1, positions), f32),
        ),
        in_specs=[SMEM] * 4 + [VMEM] * 2,
        out_specs=(VMEM,) * 3,
        scratch_shapes=[pltpu.VMEM((planes, tile, tile + W), f32)],
        compiler_params=params,
        name="deposit",
    )(scan_rows, scan_columns, section_counts, tick_order, pulls, arrived)
    incoming = moved(overflow, "lat", 1)
    slice_grad = pl.pallas_call(
        merge_kernel,
        out_shape=jax.ShapeDtypeStruct((slots, 2, tile, tile), f32),
        in_specs=[VMEM] * 2,
        out_specs=VMEM,
        compiler_params=params,
        name="merge",
    )(main, incoming)
    return slice_grad, losses


def solution(mesh):
    placed = (
        P("depth", None, None, "lat"),
        P("depth"),
        P("lat"),
        P("lat"),
        P("lat", None),
        P("lat", None, None),
        P(),
    )
    return jax.shard_map(
        shards,
        mesh=mesh,
        in_specs=placed,
        out_specs=(P("depth", None, None, "lat"), P("lat", None)),
        check_vma=False,
    )
```

```python
import functools

import jax
import jax.numpy as jnp
import numpy as np
from jax import lax
from jax.experimental import pallas as pl
from jax.experimental.pallas import tpu as pltpu
from jax.sharding import PartitionSpec as P


FRESNEL = 12.0
W = 128
f32 = jnp.float32
bf16 = jnp.bfloat16
ORDER = 16
COUNT = 24
PLACE = 25


def moved(block, axis, distance):
    count = lax.axis_size(axis)
    return lax.ppermute(block, axis, [((i - distance) % count, i) for i in range(count)])


def swapped(block):
    count = lax.axis_size("depth")
    return lax.ppermute(block, "depth", [(i ^ 1, i) for i in range(count)])


def three_parts(array):
    parts = []
    rest = np.asarray(array, np.float64)
    for _ in range(3):
        part = rest.astype(np.float32).astype(bf16)
        parts.append(part)
        rest = rest - part.astype(np.float64)
    return parts


def right_table(matrix):
    first, second, third = three_parts(np.concatenate([matrix.real, matrix.imag], 1))
    return np.concatenate([first, first, second, third], 0)


def left_table(matrix):
    first, second, third = three_parts(np.concatenate([matrix.real, matrix.imag], 0))
    return np.concatenate(
        [np.concatenate([first, first], 1), np.concatenate([second, third], 1)], 0
    )


def make_tables(width):
    index = np.arange(width)
    fourier = np.exp(-2j * np.pi * (np.outer(index, index) % width) / width) / np.sqrt(width)
    frequency = ((index + width // 2) % width - width // 2) / width
    chirp = np.exp(-1j * FRESNEL * frequency * frequency)
    step = np.conj(fourier) @ (chirp[:, None] * fourier)
    return tuple(make(matrix) for matrix in (step, fourier) for make in (right_table, left_table))


def halves(value):
    high = value.astype(bf16)
    return high, (value - high.astype(f32)).astype(bf16)


def product(a, b):
    return jnp.dot(a, b, preferred_element_type=f32)


def spread_out(part, right):
    high, low = halves(part)
    return product(jnp.concatenate([high, low, high, high], 1), right)


def combined(z, conjugate):
    if conjugate:
        return jnp.concatenate([z[0][:, :W] + z[1][:, W:], z[1][:, :W] - z[0][:, W:]], 1)
    return jnp.concatenate([z[0][:, :W] - z[1][:, W:], z[0][:, W:] + z[1][:, :W]], 1)


def two_sided(real, imag, right, left, conjugate):
    y = combined([spread_out(part, right) for part in (real, imag)], conjugate)
    high, low = halves(y)
    z = product(left[: 2 * W], jnp.concatenate([high, low], 0)) + product(
        left[2 * W :], jnp.concatenate([high, high], 0)
    )
    if conjugate:
        return z[:W, :W] + z[W:, W:], z[:W, W:] - z[W:, :W]
    return z[:W, :W] - z[W:, W:], z[:W, W:] + z[W:, :W]


def at_window(meta, p, tile):
    positions = 8
    row = pl.multiple_of(jnp.minimum(meta[p] // 8 * 8, tile - W - 8), 8)
    block = jnp.minimum(meta[positions + p] // W, tile // W - 1)
    start = pl.multiple_of(block * W, W)
    after = pl.multiple_of(block * W + W, W)
    return row, meta[p] - row, start, after, meta[positions + p] - block * W


def cut_kernel(meta, own, rim, out, extended, *, base):
    slots = rim.shape[0]
    positions = out.shape[0]
    tile = own.shape[3]
    for slot in range(slots):
        for part in range(2):
            extended[2 * slot + part, :, :tile] = own[base + slot, part]
            extended[2 * slot + part, :, tile:] = rim[slot, part]
    lane = lax.broadcasted_iota(jnp.int32, (W + 8, W), 1)
    stamp = jnp.full((8, W), meta[COUNT], jnp.int32).astype(f32)

    def one_position(p, carry):
        row, drop, start, after, shift = at_window(meta, p, tile)
        lift = (W + 8 - drop) % (W + 8)
        turn = (W - shift) % W
        for plane in range(2 * slots):
            first = extended[plane, pl.ds(row, W + 8), pl.ds(start, W)]
            second = extended[plane, pl.ds(row, W + 8), pl.ds(after, W)]
            both = jnp.where(
                lane < W - shift, pltpu.roll(first, turn, 1), pltpu.roll(second, turn, 1)
            )
            out[p, plane * W : (plane + 1) * W, :] = pltpu.roll(both, lift, 0)[:W]
        if base == 0:
            out[p, 2 * slots * W :, :] = stamp
        return carry

    lax.fori_loop(0, positions, one_position, 0)


def two_sided_each(fields, right, left, conjugate):
    every = [
        spread_out(jnp.concatenate([field[part] for field in fields], 0), right) for part in range(2)
    ]
    results = []
    for index in range(len(fields)):
        y = combined([z[index * W : index * W + W] for z in every], conjugate)
        high, low = halves(y)
        z = product(left[: 2 * W], jnp.concatenate([high, low], 0)) + product(
            left[2 * W :], jnp.concatenate([high, high], 0)
        )
        if conjugate:
            results.append((z[:W, :W] + z[W:, W:], z[:W, W:] - z[W:, :W]))
        else:
            results.append((z[:W, :W] - z[W:, W:], z[:W, W:] + z[W:, :W]))
    return results


def times(a, b):
    return a[0] * b[0] - a[1] * b[1], a[0] * b[1] + a[1] * b[0]


def times_conjugate(a, b):
    return a[0] * b[0] + a[1] * b[1], a[0] * b[1] - a[1] * b[0]


def wave_kernel(
    meta,
    mine_zero,
    other_zero,
    mine_rest,
    other_rest,
    measured,
    illumination,
    step_right,
    step_left,
    far_right,
    far_left,
    out,
    counts,
):
    chips = mine_zero.shape[0]
    sections = 2 * chips
    core = meta[PLACE] % 2
    for chip in range(chips):
        own = jnp.max(mine_zero[chip, 2 * W :, :]).astype(jnp.int32)
        its = jnp.max(other_zero[chip, 2 * W :, :]).astype(jnp.int32)
        counts[2 * chip] = jnp.where(core == 0, own, its)
        counts[2 * chip + 1] = jnp.where(core == 0, its, own)

    def zero_window(section):
        chip = section // 2
        local = section % 2 == core
        return tuple(
            jnp.where(
                local,
                mine_zero[chip, part * W : part * W + W, :],
                other_zero[chip, part * W : part * W + W, :],
            )
            for part in range(2)
        )

    def rest_window(section, slot):
        chip = section // 2
        local = section % 2 == core
        at = pl.multiple_of((slot - 1) * 2 * W, 2 * W)
        return tuple(
            jnp.where(
                local,
                mine_rest[chip, pl.ds(at + part * W, W), :],
                other_rest[chip, pl.ds(at + part * W, W), :],
            )
            for part in range(2)
        )

    def any_window(section, slot):
        pairs = zip(zero_window(section), rest_window(section, jnp.maximum(slot, 1)))
        return tuple(jnp.where(slot == 0, a, b) for a, b in pairs)

    def keep(chip, field):
        out[chip, :W, :] = field[0]
        out[chip, W : 2 * W, :] = field[1]

    def ahead(field, window):
        return two_sided(*times(field, window), step_right[...], step_left[...], False)

    def back(field, window):
        return times_conjugate(window, two_sided(*field, step_right[...], step_left[...], True))

    def forward_section(section, field):
        @pl.when((core == 0) & (section % 2 == 0))
        def _():
            keep(section // 2, field)

        field = ahead(field, zero_window(section))
        return lax.fori_loop(
            1, counts[section], lambda slot, value: ahead(value, rest_window(section, slot)), field
        )

    def backward_section(index, field):
        section = sections - 2 - index

        @pl.when(section % 2 == 1)
        def _():
            keep(section // 2, field)

        count = counts[section]
        field = lax.fori_loop(
            1, count, lambda step, value: back(value, rest_window(section, count - step)), field
        )
        return back(field, zero_window(section))

    last = sections - 1
    final = counts[last] - 1
    field = lax.fori_loop(0, last, forward_section, (illumination[0], illumination[1]))
    field = lax.fori_loop(
        0, final, lambda slot, value: ahead(value, any_window(last, slot)), field
    )
    field = times(field, any_window(last, final))
    real, imag = two_sided(*field, far_right[...], far_left[...], False)
    misfit = real * real + imag * imag - measured[meta[PLACE] // 2]
    loss = jnp.sum(misfit * misfit) * (1.0 / (W * W))
    for chip in range(chips):
        out[chip, 2 * W :, :] = jnp.full((8, W), loss, f32)

    @pl.when(core == 1)
    def _():
        spread = two_sided(
            4.0 * misfit * real, 4.0 * misfit * imag, far_right[...], far_left[...], True
        )
        keep(chips - 1, spread)
        value = times_conjugate(any_window(last, final), spread)
        value = lax.fori_loop(
            0, final, lambda step, value: back(value, any_window(last, final - 1 - step)), value
        )
        keep(0, lax.fori_loop(0, sections - 3, backward_section, value))


GROUP = 4


def fields_of(ref, group, at):
    return [
        tuple(ref[group * GROUP + each, pl.ds(at + part * W, W), :] for part in range(2))
        for each in range(GROUP)
    ]


def put_fields(ref, group, at, fields):
    for each in range(GROUP):
        for part in range(2):
            ref[group * GROUP + each, pl.ds(at + part * W, W), :] = fields[each][part]


def window_of(zero, rest, group, slot):
    at = pl.multiple_of(jnp.maximum(slot - 1, 0) * 2 * W, 2 * W)
    return [
        tuple(jnp.where(slot == 0, a, b) for a, b in zip(*pair))
        for pair in zip(fields_of(zero, group, 0), fields_of(rest, group, at))
    ]


def first_kernel(meta, zero, rest, arrived, step_right, step_left, track, handed):
    core = meta[PLACE] % 2
    top = meta[COUNT]
    groups = zero.shape[0] // GROUP
    sections = 2 * zero.shape[0]

    @pl.when(core == 0)
    def _():
        def one_group(group, carry):
            put_fields(handed, group, 0, fields_of(arrived, group, 0))

            def one(slot, inner):
                at = pl.multiple_of(slot * 2 * W, 2 * W)
                fields = fields_of(handed, group, 0)
                put_fields(track, group, at, fields)
                cut = window_of(zero, rest, group, slot)
                fields = [times(a, b) for a, b in zip(fields, cut)]
                put_fields(
                    handed, group, 0, two_sided_each(fields, step_right[...], step_left[...], False)
                )
                return inner

            return lax.fori_loop(0, top, one, carry)

        lax.fori_loop(0, groups, one_group, 0)

    @pl.when(core == 1)
    def _():
        def one_group(group, carry):
            put_fields(handed, group, 0, fields_of(arrived, group, 0))

            def one(step, inner):
                at = pl.multiple_of((top - 1 - step) * 2 * W, 2 * W)
                fields = fields_of(handed, group, 0)
                spread = two_sided_each(fields, step_right[...], step_left[...], True)
                done = (step == 0) & (meta[PLACE] == sections - 1)
                spread = [
                    tuple(jnp.where(done, kept, fresh) for kept, fresh in zip(a, b))
                    for a, b in zip(fields, spread)
                ]
                put_fields(track, group, at, spread)
                cut = window_of(zero, rest, group, top - 1 - step)
                put_fields(handed, group, 0, [times_conjugate(a, b) for a, b in zip(cut, spread)])
                return inner

            return lax.fori_loop(0, top, one, carry)

        lax.fori_loop(0, groups, one_group, 0)


def second_kernel(
    meta, zero, rest, track, handed, arrived, step_right, step_left, main, rim, losses, pulls, state, total
):
    core = meta[PLACE] % 2
    top = meta[COUNT]
    groups = zero.shape[0] // GROUP

    @pl.when(core == 0)
    def _():
        def one_group(group, carry):
            put_fields(state, group, 0, fields_of(handed, group, 0))

            def one(step, inner):
                at = pl.multiple_of((top - 1 - step) * 2 * W, 2 * W)
                fields = fields_of(state, group, 0)
                spread = two_sided_each(fields, step_right[...], step_left[...], True)
                waves = fields_of(track, group, at)
                put_fields(pulls, group, at, [times_conjugate(a, b) for a, b in zip(waves, spread)])
                cut = window_of(zero, rest, group, top - 1 - step)
                put_fields(state, group, 0, [times_conjugate(a, b) for a, b in zip(cut, spread)])
                return inner

            return lax.fori_loop(0, top, one, carry)

        lax.fori_loop(0, groups, one_group, 0)

    @pl.when(core == 1)
    def _():
        def one_group(group, carry):
            put_fields(state, group, 0, fields_of(handed, group, 0))

            def pull(slot):
                at = pl.multiple_of(slot * 2 * W, 2 * W)
                fields = fields_of(state, group, 0)
                spread = fields_of(track, group, at)
                put_fields(pulls, group, at, [times_conjugate(a, b) for a, b in zip(fields, spread)])
                return fields

            def one(slot, inner):
                fields = pull(slot)
                cut = window_of(zero, rest, group, slot)
                fields = [times(a, b) for a, b in zip(fields, cut)]
                put_fields(
                    state, group, 0, two_sided_each(fields, step_right[...], step_left[...], False)
                )
                return inner

            lax.fori_loop(0, top - 1, one, carry)
            pull(top - 1)
            return carry

        lax.fori_loop(0, groups, one_group, 0)

    deposit(meta, pulls, arrived, main, rim, losses, total)


def deposit(meta, pulls, arrived, main, rim, losses, total):
    positions = pulls.shape[0]
    planes = pulls.shape[1] // W
    tile = main.shape[3]
    total[...] = jnp.zeros_like(total)
    lane = lax.broadcasted_iota(jnp.int32, (W + 8, W), 1)
    spare = jnp.zeros((8, W), f32)

    def one_position(p, carry):
        row, drop, start, after, shift = at_window(meta, p, tile)

        def one_slot(slot, inner):
            for part in range(2):
                at = pl.multiple_of((2 * slot + part) * W, W)
                pull = jnp.concatenate([pulls[p, pl.ds(at, W), :], spare], 0)
                pull = pltpu.roll(pltpu.roll(pull, drop, 0), shift % W, 1)
                plane = 2 * slot + part
                total[plane, pl.ds(row, W + 8), pl.ds(start, W)] += jnp.where(lane >= shift, pull, 0.0)
                total[plane, pl.ds(row, W + 8), pl.ds(after, W)] += jnp.where(lane < shift, pull, 0.0)
            return inner

        return lax.fori_loop(0, meta[COUNT], one_slot, carry)

    lax.fori_loop(0, positions, one_position, 0)
    for plane in range(planes):
        main[plane // 2, plane % 2] = total[plane, :, :tile]
        rim[plane // 2, plane % 2] = total[plane, :, tile:]
    place = lax.broadcasted_iota(jnp.int32, (1, W), 1)
    line = jnp.zeros((1, W), f32)
    for j in range(positions):
        line = jnp.where(place == j, arrived[meta[ORDER + j], 2 * W : 2 * W + 1, :], line)
    losses[...] = line[:, :positions]


def merge_kernel(main, rim, out):
    out[:, :, :, W:] = main[:, :, :, W:]
    out[:, :, :, :W] = main[:, :, :, :W] + rim[...]


VMEM = pl.BlockSpec(memory_space=pltpu.VMEM)
SMEM = pl.BlockSpec(memory_space=pltpu.SMEM)


def shards(slices, section_counts, scan_rows, scan_columns, tick_order, measured, illumination):
    slots = slices.shape[0]
    tile = slices.shape[3]
    positions = scan_rows.shape[0]
    planes = 2 * slots
    chips = lax.axis_size("depth") // 2
    place = lax.axis_index("depth")
    groups = [[2 * chip + core for chip in range(chips)] for core in range(2)]
    exchange = functools.partial(
        lax.all_to_all, axis_name="depth", split_axis=0, concat_axis=0, tiled=True, axis_index_groups=groups
    )
    params = pltpu.CompilerParams(vmem_limit_bytes=24 << 20)
    tables = [jnp.asarray(table) for table in make_tables(W)]
    meta = jnp.concatenate(
        [scan_rows, scan_columns, tick_order[0], section_counts, place.reshape(1)]
    ).astype(jnp.int32)

    def cut(base, count, rim):
        return pl.pallas_call(
            functools.partial(cut_kernel, base=base),
            out_shape=jax.ShapeDtypeStruct(
                (positions, 2 * count * W + (8 if base == 0 else 0), W), f32
            ),
            in_specs=[SMEM] + [VMEM] * 2,
            out_specs=VMEM,
            scratch_shapes=[pltpu.VMEM((2 * count, tile, tile + W), f32)],
            compiler_params=params,
            name="cut",
        )(meta, slices, rim)

    rim_zero = moved(slices[:1, ..., :W], "lat", -1)
    zero = cut(0, 1, rim_zero)
    edge, zero = lax.optimization_barrier((slices[1:, ..., :W], zero))
    rim_rest = moved(edge, "lat", -1)
    mine_zero = exchange(zero)
    other_zero = swapped(mine_zero)
    rest = cut(1, slots - 1, rim_rest)
    sent, _ = lax.optimization_barrier((rest, mine_zero))
    mine_rest = exchange(sent)
    other_rest = swapped(mine_rest)
    boundary = pl.pallas_call(
        wave_kernel,
        out_shape=jax.ShapeDtypeStruct((chips, 2 * W + 8, W), f32),
        in_specs=[SMEM] + [VMEM] * 10,
        out_specs=VMEM,
        scratch_shapes=[pltpu.SMEM((2 * chips,), jnp.int32)],
        compiler_params=params,
        name="wave",
    )(meta, mine_zero, other_zero, mine_rest, other_rest, measured, illumination, *tables)
    arrived = exchange(boundary)
    track, handed = pl.pallas_call(
        first_kernel,
        out_shape=(
            jax.ShapeDtypeStruct((positions, planes * W, W), f32),
            jax.ShapeDtypeStruct((positions, 2 * W, W), f32),
        ),
        in_specs=[SMEM] + [VMEM] * 5,
        out_specs=(VMEM,) * 2,
        compiler_params=params,
        name="first",
    )(meta, zero, rest, arrived, *tables[:2])
    main, overflow, losses = pl.pallas_call(
        second_kernel,
        out_shape=(
            jax.ShapeDtypeStruct((slots, 2, tile, tile), f32),
            jax.ShapeDtypeStruct((slots, 2, tile, W), f32),
            jax.ShapeDtypeStruct((1, positions), f32),
        ),
        in_specs=[SMEM] + [VMEM] * 7,
        out_specs=(VMEM,) * 3,
        scratch_shapes=[
            pltpu.VMEM((positions, planes * W, W), f32),
            pltpu.VMEM((positions, 2 * W, W), f32),
            pltpu.VMEM((planes, tile, tile + W), f32),
        ],
        compiler_params=params,
        name="second",
    )(meta, zero, rest, track, swapped(handed), arrived, *tables[:2])
    incoming = moved(overflow, "lat", 1)
    slice_grad = pl.pallas_call(
        merge_kernel,
        out_shape=jax.ShapeDtypeStruct((slots, 2, tile, tile), f32),
        in_specs=[VMEM] * 2,
        out_specs=VMEM,
        compiler_params=params,
        name="merge",
    )(main, incoming)
    return slice_grad, losses


def solution(mesh):
    placed = (
        P("depth", None, None, "lat"),
        P("depth"),
        P("lat"),
        P("lat"),
        P("lat", None),
        P("lat", None, None),
        P(),
    )
    return jax.shard_map(
        shards,
        mesh=mesh,
        in_specs=placed,
        out_specs=(P("depth", None, None, "lat"), P("lat", None)),
        check_vma=False,
    )
```

```python
import functools

import jax
import jax.numpy as jnp
import numpy as np
from jax import lax
from jax.experimental import pallas as pl
from jax.experimental.pallas import tpu as pltpu
from jax.sharding import PartitionSpec as P


FRESNEL = 12.0
W = 128
f32 = jnp.float32
bf16 = jnp.bfloat16
ORDER = 16
COUNT = 24
PLACE = 25


def moved(block, axis, distance):
    count = lax.axis_size(axis)
    return lax.ppermute(block, axis, [((i - distance) % count, i) for i in range(count)])


def swapped(block):
    count = lax.axis_size("depth")
    return lax.ppermute(block, "depth", [(i ^ 1, i) for i in range(count)])


def three_parts(array):
    parts = []
    rest = np.asarray(array, np.float64)
    for _ in range(3):
        part = rest.astype(np.float32).astype(bf16)
        parts.append(part)
        rest = rest - part.astype(np.float64)
    return parts


def right_table(matrix):
    first, second, third = three_parts(np.concatenate([matrix.real, matrix.imag], 1))
    return np.concatenate([first, first, second, third], 0)


def left_table(matrix):
    first, second, third = three_parts(np.concatenate([matrix.real, matrix.imag], 0))
    return np.concatenate(
        [np.concatenate([first, first], 1), np.concatenate([second, third], 1)], 0
    )


def make_tables(width):
    index = np.arange(width)
    fourier = np.exp(-2j * np.pi * (np.outer(index, index) % width) / width) / np.sqrt(width)
    frequency = ((index + width // 2) % width - width // 2) / width
    chirp = np.exp(-1j * FRESNEL * frequency * frequency)
    step = np.conj(fourier) @ (chirp[:, None] * fourier)
    return tuple(make(matrix) for matrix in (step, fourier) for make in (right_table, left_table))


def halves(value):
    high = value.astype(bf16)
    return high, (value - high.astype(f32)).astype(bf16)


def product(a, b):
    return jnp.dot(a, b, preferred_element_type=f32)


def spread_out(part, right):
    high, low = halves(part)
    return product(jnp.concatenate([high, low, high, high], 1), right)


def combined(z, conjugate):
    if conjugate:
        return jnp.concatenate([z[0][:, :W] + z[1][:, W:], z[1][:, :W] - z[0][:, W:]], 1)
    return jnp.concatenate([z[0][:, :W] - z[1][:, W:], z[0][:, W:] + z[1][:, :W]], 1)


def right_of(field, right, conjugate):
    z = []
    for part in field:
        high, low = halves(part)
        z.append(
            product(jnp.concatenate([high, low], 1), right[: 2 * W])
            + product(jnp.concatenate([high, high], 1), right[2 * W :])
        )
    return combined(z, conjugate)


def left_of(y, left, conjugate):
    high, low = halves(y)
    first = jnp.concatenate([high, low], 0)
    second = jnp.concatenate([high, high], 0)
    real, imag = (
        product(left[at : at + W], first) + product(left[2 * W + at : 3 * W + at], second)
        for at in (0, W)
    )
    if conjugate:
        return real[:, :W] + imag[:, W:], real[:, W:] - imag[:, :W]
    return real[:, :W] - imag[:, W:], real[:, W:] + imag[:, :W]


def at_window(meta, p, tile):
    positions = 8
    row = pl.multiple_of(jnp.minimum(meta[p] // 8 * 8, tile - W - 8), 8)
    block = jnp.minimum(meta[positions + p] // W, tile // W - 1)
    start = pl.multiple_of(block * W, W)
    after = pl.multiple_of(block * W + W, W)
    return row, meta[p] - row, start, after, meta[positions + p] - block * W


def cut_kernel(meta, own, rim, out, extended, *, base):
    slots = rim.shape[0]
    positions = out.shape[0]
    tile = own.shape[3]
    for slot in range(slots):
        for part in range(2):
            extended[2 * slot + part, :, :tile] = own[base + slot, part]
            extended[2 * slot + part, :, tile:] = rim[slot, part]
    lane = lax.broadcasted_iota(jnp.int32, (W + 8, W), 1)
    stamp = jnp.full((8, W), meta[COUNT], jnp.int32).astype(f32)

    def one_position(p, carry):
        row, drop, start, after, shift = at_window(meta, p, tile)
        lift = (W + 8 - drop) % (W + 8)
        turn = (W - shift) % W
        for plane in range(2 * slots):
            first = extended[plane, pl.ds(row, W + 8), pl.ds(start, W)]
            second = extended[plane, pl.ds(row, W + 8), pl.ds(after, W)]
            both = jnp.where(
                lane < W - shift, pltpu.roll(first, turn, 1), pltpu.roll(second, turn, 1)
            )
            out[p, plane * W : (plane + 1) * W, :] = pltpu.roll(both, lift, 0)[:W]
        if base == 0:
            out[p, 2 * slots * W :, :] = stamp
        return carry

    lax.fori_loop(0, positions, one_position, 0)


def two_sided_each(fields, right, left, conjugate):
    every = [
        spread_out(jnp.concatenate([field[part] for field in fields], 0), right) for part in range(2)
    ]
    results = []
    for index in range(len(fields)):
        y = combined([z[index * W : index * W + W] for z in every], conjugate)
        high, low = halves(y)
        z = product(left[: 2 * W], jnp.concatenate([high, low], 0)) + product(
            left[2 * W :], jnp.concatenate([high, high], 0)
        )
        if conjugate:
            results.append((z[:W, :W] + z[W:, W:], z[:W, W:] - z[W:, :W]))
        else:
            results.append((z[:W, :W] - z[W:, W:], z[:W, W:] + z[W:, :W]))
    return results


def times(a, b):
    return a[0] * b[0] - a[1] * b[1], a[0] * b[1] + a[1] * b[0]


def times_conjugate(a, b):
    return a[0] * b[0] + a[1] * b[1], a[0] * b[1] - a[1] * b[0]


def wave_kernel(
    meta,
    mine_zero,
    other_zero,
    mine_rest,
    other_rest,
    measured,
    illumination,
    step_right,
    step_left,
    far_right,
    far_left,
    out,
    counts,
):
    chips = mine_zero.shape[0]
    sections = 2 * chips
    core = meta[PLACE] % 2
    for chip in range(chips):
        own = jnp.max(mine_zero[chip, 2 * W :, :]).astype(jnp.int32)
        its = jnp.max(other_zero[chip, 2 * W :, :]).astype(jnp.int32)
        counts[2 * chip] = jnp.where(core == 0, own, its)
        counts[2 * chip + 1] = jnp.where(core == 0, its, own)

    def zero_window(section):
        chip = section // 2
        local = section % 2 == core
        return tuple(
            jnp.where(
                local,
                mine_zero[chip, part * W : part * W + W, :],
                other_zero[chip, part * W : part * W + W, :],
            )
            for part in range(2)
        )

    def rest_window(section, slot):
        chip = section // 2
        local = section % 2 == core
        at = pl.multiple_of((slot - 1) * 2 * W, 2 * W)
        return tuple(
            jnp.where(
                local,
                mine_rest[chip, pl.ds(at + part * W, W), :],
                other_rest[chip, pl.ds(at + part * W, W), :],
            )
            for part in range(2)
        )

    def any_window(section, slot):
        pairs = zip(zero_window(section), rest_window(section, jnp.maximum(slot, 1)))
        return tuple(jnp.where(slot == 0, a, b) for a, b in pairs)

    def keep(chip, field):
        out[chip, :W, :] = field[0]
        out[chip, W : 2 * W, :] = field[1]

    def ahead(field, window):
        return right_of(times(field, window), step_right[...], False)

    def reached(y):
        return left_of(y, step_left[...], False)

    def back(y, window):
        return times_conjugate(window, left_of(y, step_left[...], True))

    def onward(field):
        return right_of(field, step_right[...], True)

    def forward_rest(section, y):
        return lax.fori_loop(
            1,
            counts[section],
            lambda slot, value: ahead(reached(value), rest_window(section, slot)),
            y,
        )

    def forward_section(section, y):
        field = reached(y)

        @pl.when((core == 0) & (section % 2 == 0))
        def _():
            keep(section // 2, field)

        return forward_rest(section, ahead(field, zero_window(section)))

    def backward_section(index, y):
        section = sections - 2 - index
        count = counts[section]
        y = lax.fori_loop(
            1, count, lambda step, value: onward(back(value, rest_window(section, count - step))), y
        )
        field = back(y, zero_window(section))

        @pl.when(section % 2 == 0)
        def _():
            keep(section // 2 - 1, field)

        return onward(field)

    last = sections - 1
    final = counts[last] - 1
    start = illumination[0], illumination[1]

    @pl.when(core == 0)
    def _():
        keep(0, start)

    y = forward_rest(0, ahead(start, zero_window(0)))
    y = lax.fori_loop(1, last, forward_section, y)
    y = lax.fori_loop(
        0, final, lambda slot, value: ahead(reached(value), any_window(last, slot)), y
    )
    field = times(reached(y), any_window(last, final))
    real, imag = left_of(right_of(field, far_right[...], False), far_left[...], False)
    misfit = real * real + imag * imag - measured[meta[PLACE] // 2]
    loss = jnp.sum(misfit * misfit) * (1.0 / (W * W))
    for chip in range(chips):
        out[chip, 2 * W :, :] = jnp.full((8, W), loss, f32)

    @pl.when(core == 1)
    def _():
        seed = 4.0 * misfit * real, 4.0 * misfit * imag
        spread = left_of(right_of(seed, far_right[...], True), far_left[...], True)
        keep(chips - 1, spread)
        y = onward(times_conjugate(any_window(last, final), spread))
        y = lax.fori_loop(
            0,
            final,
            lambda step, value: onward(back(value, any_window(last, final - 1 - step))),
            y,
        )
        lax.fori_loop(0, sections - 3, backward_section, y)


GROUP = 4


def fields_of(ref, group, at):
    return [
        tuple(ref[group * GROUP + each, pl.ds(at + part * W, W), :] for part in range(2))
        for each in range(GROUP)
    ]


def put_fields(ref, group, at, fields):
    for each in range(GROUP):
        for part in range(2):
            ref[group * GROUP + each, pl.ds(at + part * W, W), :] = fields[each][part]


def window_of(zero, rest, group, slot):
    at = pl.multiple_of(jnp.maximum(slot - 1, 0) * 2 * W, 2 * W)
    return [
        tuple(jnp.where(slot == 0, a, b) for a, b in zip(*pair))
        for pair in zip(fields_of(zero, group, 0), fields_of(rest, group, at))
    ]


def first_kernel(meta, zero, rest, arrived, step_right, step_left, track, handed):
    core = meta[PLACE] % 2
    top = meta[COUNT]
    groups = zero.shape[0] // GROUP
    sections = 2 * zero.shape[0]

    @pl.when(core == 0)
    def _():
        def one_group(group, carry):
            put_fields(handed, group, 0, fields_of(arrived, group, 0))

            def one(slot, inner):
                at = pl.multiple_of(slot * 2 * W, 2 * W)
                fields = fields_of(handed, group, 0)
                put_fields(track, group, at, fields)
                cut = window_of(zero, rest, group, slot)
                fields = [times(a, b) for a, b in zip(fields, cut)]
                put_fields(
                    handed, group, 0, two_sided_each(fields, step_right[...], step_left[...], False)
                )
                return inner

            return lax.fori_loop(0, top, one, carry)

        lax.fori_loop(0, groups, one_group, 0)

    @pl.when(core == 1)
    def _():
        def one_group(group, carry):
            put_fields(handed, group, 0, fields_of(arrived, group, 0))

            def one(step, inner):
                at = pl.multiple_of((top - 1 - step) * 2 * W, 2 * W)
                fields = fields_of(handed, group, 0)
                spread = two_sided_each(fields, step_right[...], step_left[...], True)
                done = (step == 0) & (meta[PLACE] == sections - 1)
                spread = [
                    tuple(jnp.where(done, kept, fresh) for kept, fresh in zip(a, b))
                    for a, b in zip(fields, spread)
                ]
                put_fields(track, group, at, spread)
                cut = window_of(zero, rest, group, top - 1 - step)
                put_fields(handed, group, 0, [times_conjugate(a, b) for a, b in zip(cut, spread)])
                return inner

            return lax.fori_loop(0, top, one, carry)

        lax.fori_loop(0, groups, one_group, 0)


def second_kernel(
    meta, zero, rest, track, handed, arrived, step_right, step_left, main, rim, losses, pulls, state, total
):
    core = meta[PLACE] % 2
    top = meta[COUNT]
    groups = zero.shape[0] // GROUP

    @pl.when(core == 0)
    def _():
        def one_group(group, carry):
            put_fields(state, group, 0, fields_of(handed, group, 0))

            def one(step, inner):
                at = pl.multiple_of((top - 1 - step) * 2 * W, 2 * W)
                fields = fields_of(state, group, 0)
                spread = two_sided_each(fields, step_right[...], step_left[...], True)
                waves = fields_of(track, group, at)
                put_fields(pulls, group, at, [times_conjugate(a, b) for a, b in zip(waves, spread)])
                cut = window_of(zero, rest, group, top - 1 - step)
                put_fields(state, group, 0, [times_conjugate(a, b) for a, b in zip(cut, spread)])
                return inner

            return lax.fori_loop(0, top, one, carry)

        lax.fori_loop(0, groups, one_group, 0)

    @pl.when(core == 1)
    def _():
        def one_group(group, carry):
            put_fields(state, group, 0, fields_of(handed, group, 0))

            def pull(slot):
                at = pl.multiple_of(slot * 2 * W, 2 * W)
                fields = fields_of(state, group, 0)
                spread = fields_of(track, group, at)
                put_fields(pulls, group, at, [times_conjugate(a, b) for a, b in zip(fields, spread)])
                return fields

            def one(slot, inner):
                fields = pull(slot)
                cut = window_of(zero, rest, group, slot)
                fields = [times(a, b) for a, b in zip(fields, cut)]
                put_fields(
                    state, group, 0, two_sided_each(fields, step_right[...], step_left[...], False)
                )
                return inner

            lax.fori_loop(0, top - 1, one, carry)
            pull(top - 1)
            return carry

        lax.fori_loop(0, groups, one_group, 0)

    deposit(meta, pulls, arrived, main, rim, losses, total)


def deposit(meta, pulls, arrived, main, rim, losses, total):
    positions = pulls.shape[0]
    planes = pulls.shape[1] // W
    tile = main.shape[3]
    total[...] = jnp.zeros_like(total)
    lane = lax.broadcasted_iota(jnp.int32, (W + 8, W), 1)
    spare = jnp.zeros((8, W), f32)

    def one_position(p, carry):
        row, drop, start, after, shift = at_window(meta, p, tile)

        def one_slot(slot, inner):
            for part in range(2):
                at = pl.multiple_of((2 * slot + part) * W, W)
                pull = jnp.concatenate([pulls[p, pl.ds(at, W), :], spare], 0)
                pull = pltpu.roll(pltpu.roll(pull, drop, 0), shift % W, 1)
                plane = 2 * slot + part
                total[plane, pl.ds(row, W + 8), pl.ds(start, W)] += jnp.where(lane >= shift, pull, 0.0)
                total[plane, pl.ds(row, W + 8), pl.ds(after, W)] += jnp.where(lane < shift, pull, 0.0)
            return inner

        return lax.fori_loop(0, meta[COUNT], one_slot, carry)

    lax.fori_loop(0, positions, one_position, 0)
    for plane in range(planes):
        main[plane // 2, plane % 2] = total[plane, :, :tile]
        rim[plane // 2, plane % 2] = total[plane, :, tile:]
    place = lax.broadcasted_iota(jnp.int32, (1, W), 1)
    line = jnp.zeros((1, W), f32)
    for j in range(positions):
        line = jnp.where(place == j, arrived[meta[ORDER + j], 2 * W : 2 * W + 1, :], line)
    losses[...] = line[:, :positions]


def merge_kernel(main, rim, out):
    out[:, :, :, W:] = main[:, :, :, W:]
    out[:, :, :, :W] = main[:, :, :, :W] + rim[...]


VMEM = pl.BlockSpec(memory_space=pltpu.VMEM)
SMEM = pl.BlockSpec(memory_space=pltpu.SMEM)


def shards(slices, section_counts, scan_rows, scan_columns, tick_order, measured, illumination):
    slots = slices.shape[0]
    tile = slices.shape[3]
    positions = scan_rows.shape[0]
    planes = 2 * slots
    chips = lax.axis_size("depth") // 2
    place = lax.axis_index("depth")
    groups = [[2 * chip + core for chip in range(chips)] for core in range(2)]
    exchange = functools.partial(
        lax.all_to_all, axis_name="depth", split_axis=0, concat_axis=0, tiled=True, axis_index_groups=groups
    )
    params = pltpu.CompilerParams(vmem_limit_bytes=24 << 20)
    tables = [jnp.asarray(table) for table in make_tables(W)]
    meta = jnp.concatenate(
        [scan_rows, scan_columns, tick_order[0], section_counts, place.reshape(1)]
    ).astype(jnp.int32)

    def cut(base, count, rim):
        return pl.pallas_call(
            functools.partial(cut_kernel, base=base),
            out_shape=jax.ShapeDtypeStruct(
                (positions, 2 * count * W + (8 if base == 0 else 0), W), f32
            ),
            in_specs=[SMEM] + [VMEM] * 2,
            out_specs=VMEM,
            scratch_shapes=[pltpu.VMEM((2 * count, tile, tile + W), f32)],
            compiler_params=params,
            name="cut",
        )(meta, slices, rim)

    rim_zero = moved(slices[:1, ..., :W], "lat", -1)
    zero = cut(0, 1, rim_zero)
    edge, zero = lax.optimization_barrier((slices[1:, ..., :W], zero))
    rim_rest = moved(edge, "lat", -1)
    mine_zero = exchange(zero)
    other_zero = swapped(mine_zero)
    rest = cut(1, slots - 1, rim_rest)
    sent, _ = lax.optimization_barrier((rest, mine_zero))
    mine_rest = exchange(sent)
    other_rest = swapped(mine_rest)
    boundary = pl.pallas_call(
        wave_kernel,
        out_shape=jax.ShapeDtypeStruct((chips, 2 * W + 8, W), f32),
        in_specs=[SMEM] + [VMEM] * 10,
        out_specs=VMEM,
        scratch_shapes=[pltpu.SMEM((2 * chips,), jnp.int32)],
        compiler_params=params,
        name="wave",
    )(meta, mine_zero, other_zero, mine_rest, other_rest, measured, illumination, *tables)
    arrived = exchange(boundary)
    track, handed = pl.pallas_call(
        first_kernel,
        out_shape=(
            jax.ShapeDtypeStruct((positions, planes * W, W), f32),
            jax.ShapeDtypeStruct((positions, 2 * W, W), f32),
        ),
        in_specs=[SMEM] + [VMEM] * 5,
        out_specs=(VMEM,) * 2,
        compiler_params=params,
        name="first",
    )(meta, zero, rest, arrived, *tables[:2])
    main, overflow, losses = pl.pallas_call(
        second_kernel,
        out_shape=(
            jax.ShapeDtypeStruct((slots, 2, tile, tile), f32),
            jax.ShapeDtypeStruct((slots, 2, tile, W), f32),
            jax.ShapeDtypeStruct((1, positions), f32),
        ),
        in_specs=[SMEM] + [VMEM] * 7,
        out_specs=(VMEM,) * 3,
        scratch_shapes=[
            pltpu.VMEM((positions, planes * W, W), f32),
            pltpu.VMEM((positions, 2 * W, W), f32),
            pltpu.VMEM((planes, tile, tile + W), f32),
        ],
        compiler_params=params,
        name="second",
    )(meta, zero, rest, track, swapped(handed), arrived, *tables[:2])
    incoming = moved(overflow, "lat", 1)
    slice_grad = pl.pallas_call(
        merge_kernel,
        out_shape=jax.ShapeDtypeStruct((slots, 2, tile, tile), f32),
        in_specs=[VMEM] * 2,
        out_specs=VMEM,
        compiler_params=params,
        name="merge",
    )(main, incoming)
    return slice_grad, losses


def solution(mesh):
    placed = (
        P("depth", None, None, "lat"),
        P("depth"),
        P("lat"),
        P("lat"),
        P("lat", None),
        P("lat", None, None),
        P(),
    )
    return jax.shard_map(
        shards,
        mesh=mesh,
        in_specs=placed,
        out_specs=(P("depth", None, None, "lat"), P("lat", None)),
        check_vma=False,
    )
```

```python
import functools

import jax
import jax.numpy as jnp
import numpy as np
from jax import lax
from jax.experimental import pallas as pl
from jax.experimental.pallas import tpu as pltpu
from jax.sharding import PartitionSpec as P


FRESNEL = 12.0
W = 128
f32 = jnp.float32
bf16 = jnp.bfloat16
ORDER = 16
COUNT = 24
PLACE = 25


def moved(block, axis, distance):
    count = lax.axis_size(axis)
    return lax.ppermute(block, axis, [((i - distance) % count, i) for i in range(count)])


def swapped(block):
    count = lax.axis_size("depth")
    return lax.ppermute(block, "depth", [(i ^ 1, i) for i in range(count)])


def three_parts(array):
    parts = []
    rest = np.asarray(array, np.float64)
    for _ in range(3):
        part = rest.astype(np.float32).astype(bf16)
        parts.append(part)
        rest = rest - part.astype(np.float64)
    return parts


def right_table(matrix):
    first, second, third = three_parts(np.concatenate([matrix.real, matrix.imag], 1))
    return np.concatenate([first, first, second, third], 0)


def left_table(matrix):
    first, second, third = three_parts(np.concatenate([matrix.real, matrix.imag], 0))
    return np.concatenate(
        [np.concatenate([first, first], 1), np.concatenate([second, third], 1)], 0
    )


def make_tables(width):
    index = np.arange(width)
    fourier = np.exp(-2j * np.pi * (np.outer(index, index) % width) / width) / np.sqrt(width)
    frequency = ((index + width // 2) % width - width // 2) / width
    chirp = np.exp(-1j * FRESNEL * frequency * frequency)
    step = np.conj(fourier) @ (chirp[:, None] * fourier)
    return tuple(make(matrix) for matrix in (step, fourier) for make in (right_table, left_table))


def halves(value):
    high = value.astype(bf16)
    return high, (value - high.astype(f32)).astype(bf16)


def product(a, b):
    return jnp.dot(a, b, preferred_element_type=f32)


def spread_out(part, right):
    high, low = halves(part)
    return product(jnp.concatenate([high, low, high, high], 1), right)


def combined(z, conjugate):
    if conjugate:
        return jnp.concatenate([z[0][:, :W] + z[1][:, W:], z[1][:, :W] - z[0][:, W:]], 1)
    return jnp.concatenate([z[0][:, :W] - z[1][:, W:], z[0][:, W:] + z[1][:, :W]], 1)


def right_of(field, right, conjugate):
    z = []
    for part in field:
        high, low = halves(part)
        z.append(
            product(jnp.concatenate([high, low], 1), right[: 2 * W])
            + product(jnp.concatenate([high, high], 1), right[2 * W :])
        )
    return combined(z, conjugate)


def left_of(y, left, conjugate):
    high, low = halves(y)
    first = jnp.concatenate([high, low], 0)
    second = jnp.concatenate([high, high], 0)
    real, imag = (
        product(left[at : at + W], first) + product(left[2 * W + at : 3 * W + at], second)
        for at in (0, W)
    )
    if conjugate:
        return real[:, :W] + imag[:, W:], real[:, W:] - imag[:, :W]
    return real[:, :W] - imag[:, W:], real[:, W:] + imag[:, :W]


def at_window(meta, p, tile):
    positions = 8
    row = pl.multiple_of(jnp.minimum(meta[p] // 8 * 8, tile - W - 8), 8)
    block = jnp.minimum(meta[positions + p] // W, tile // W - 1)
    start = pl.multiple_of(block * W, W)
    after = pl.multiple_of(block * W + W, W)
    return row, meta[p] - row, start, after, meta[positions + p] - block * W


def cut_kernel(meta, own, rim, out, extended, *, base):
    slots = rim.shape[0]
    positions = out.shape[0]
    tile = own.shape[3]
    for slot in range(slots):
        for part in range(2):
            extended[2 * slot + part, :, :tile] = own[base + slot, part]
            extended[2 * slot + part, :, tile:] = rim[slot, part]
    lane = lax.broadcasted_iota(jnp.int32, (W + 8, W), 1)
    stamp = jnp.full((8, W), meta[COUNT], jnp.int32).astype(f32)

    def one_position(p, carry):
        row, drop, start, after, shift = at_window(meta, p, tile)
        lift = (W + 8 - drop) % (W + 8)
        turn = (W - shift) % W
        for plane in range(2 * slots):
            first = extended[plane, pl.ds(row, W + 8), pl.ds(start, W)]
            second = extended[plane, pl.ds(row, W + 8), pl.ds(after, W)]
            both = jnp.where(
                lane < W - shift, pltpu.roll(first, turn, 1), pltpu.roll(second, turn, 1)
            )
            out[p, plane * W : (plane + 1) * W, :] = pltpu.roll(both, lift, 0)[:W]
        if base == 0:
            out[p, 2 * slots * W :, :] = stamp
        return carry

    lax.fori_loop(0, positions, one_position, 0)


def two_sided_each(fields, right, left, conjugate):
    every = [
        spread_out(jnp.concatenate([field[part] for field in fields], 0), right) for part in range(2)
    ]
    results = []
    for index in range(len(fields)):
        y = combined([z[index * W : index * W + W] for z in every], conjugate)
        high, low = halves(y)
        z = product(left[: 2 * W], jnp.concatenate([high, low], 0)) + product(
            left[2 * W :], jnp.concatenate([high, high], 0)
        )
        if conjugate:
            results.append((z[:W, :W] + z[W:, W:], z[:W, W:] - z[W:, :W]))
        else:
            results.append((z[:W, :W] - z[W:, W:], z[:W, W:] + z[W:, :W]))
    return results


def times(a, b):
    return a[0] * b[0] - a[1] * b[1], a[0] * b[1] + a[1] * b[0]


def times_conjugate(a, b):
    return a[0] * b[0] + a[1] * b[1], a[0] * b[1] - a[1] * b[0]


def wave_kernel(
    meta,
    mine_zero,
    other_zero,
    mine_rest,
    other_rest,
    measured,
    illumination,
    step_right,
    step_left,
    far_right,
    far_left,
    out,
    counts,
):
    chips = mine_zero.shape[0]
    sections = 2 * chips
    core = meta[PLACE] % 2
    for chip in range(chips):
        own = jnp.max(mine_zero[chip, 2 * W :, :]).astype(jnp.int32)
        its = jnp.max(other_zero[chip, 2 * W :, :]).astype(jnp.int32)
        counts[2 * chip] = jnp.where(core == 0, own, its)
        counts[2 * chip + 1] = jnp.where(core == 0, its, own)

    def zero_window(section):
        chip = section // 2
        local = section % 2 == core
        return tuple(
            jnp.where(
                local,
                mine_zero[chip, part * W : part * W + W, :],
                other_zero[chip, part * W : part * W + W, :],
            )
            for part in range(2)
        )

    def rest_window(section, slot):
        chip = section // 2
        local = section % 2 == core
        at = pl.multiple_of((slot - 1) * 2 * W, 2 * W)
        return tuple(
            jnp.where(
                local,
                mine_rest[chip, pl.ds(at + part * W, W), :],
                other_rest[chip, pl.ds(at + part * W, W), :],
            )
            for part in range(2)
        )

    def any_window(section, slot):
        pairs = zip(zero_window(section), rest_window(section, jnp.maximum(slot, 1)))
        return tuple(jnp.where(slot == 0, a, b) for a, b in pairs)

    def keep(chip, field):
        out[chip, :W, :] = field[0]
        out[chip, W : 2 * W, :] = field[1]

    def ahead(field, window):
        return right_of(times(field, window), step_right[...], False)

    def reached(y):
        return left_of(y, step_left[...], False)

    def back(y, window):
        return times_conjugate(window, left_of(y, step_left[...], True))

    def onward(field):
        return right_of(field, step_right[...], True)

    def forward_rest(section, y):
        return lax.fori_loop(
            1,
            counts[section],
            lambda slot, value: ahead(reached(value), rest_window(section, slot)),
            y,
        )

    def forward_section(section, y):
        field = reached(y)

        @pl.when((core == 0) & (section % 2 == 0))
        def _():
            keep(section // 2, field)

        return forward_rest(section, ahead(field, zero_window(section)))

    def backward_section(index, y):
        section = sections - 2 - index
        count = counts[section]
        y = lax.fori_loop(
            1, count, lambda step, value: onward(back(value, rest_window(section, count - step))), y
        )
        field = back(y, zero_window(section))

        @pl.when(section % 2 == 0)
        def _():
            keep(section // 2 - 1, field)

        return onward(field)

    last = sections - 1
    final = counts[last] - 1
    start = illumination[0], illumination[1]

    @pl.when(core == 0)
    def _():
        keep(0, start)

    y = forward_rest(0, ahead(start, zero_window(0)))
    y = lax.fori_loop(1, last, forward_section, y)
    y = lax.fori_loop(
        0, final, lambda slot, value: ahead(reached(value), any_window(last, slot)), y
    )
    field = times(reached(y), any_window(last, final))
    real, imag = left_of(right_of(field, far_right[...], False), far_left[...], False)
    misfit = real * real + imag * imag - measured[meta[PLACE] // 2]
    loss = jnp.sum(misfit * misfit) * (1.0 / (W * W))
    for chip in range(chips):
        out[chip, 2 * W :, :] = jnp.full((8, W), loss, f32)

    @pl.when(core == 1)
    def _():
        seed = 4.0 * misfit * real, 4.0 * misfit * imag
        spread = left_of(right_of(seed, far_right[...], True), far_left[...], True)
        keep(chips - 1, spread)
        y = onward(times_conjugate(any_window(last, final), spread))
        y = lax.fori_loop(
            0,
            final,
            lambda step, value: onward(back(value, any_window(last, final - 1 - step))),
            y,
        )
        lax.fori_loop(0, sections - 3, backward_section, y)


GROUP = 4


def fields_of(ref, group, at):
    return [
        tuple(ref[group * GROUP + each, pl.ds(at + part * W, W), :] for part in range(2))
        for each in range(GROUP)
    ]


def put_fields(ref, group, at, fields):
    for each in range(GROUP):
        for part in range(2):
            ref[group * GROUP + each, pl.ds(at + part * W, W), :] = fields[each][part]


def window_of(zero, rest, group, slot):
    at = pl.multiple_of(jnp.maximum(slot - 1, 0) * 2 * W, 2 * W)
    return [
        tuple(jnp.where(slot == 0, a, b) for a, b in zip(*pair))
        for pair in zip(fields_of(zero, group, 0), fields_of(rest, group, at))
    ]


def first_kernel(meta, zero, rest, arrived, step_right, step_left, track, handed):
    core = meta[PLACE] % 2
    top = meta[COUNT]
    groups = zero.shape[0] // GROUP
    sections = 2 * zero.shape[0]

    @pl.when(core == 0)
    def _():
        def one_group(group, carry):
            put_fields(handed, group, 0, fields_of(arrived, group, 0))

            def one(slot, inner):
                at = pl.multiple_of(slot * 2 * W, 2 * W)
                fields = fields_of(handed, group, 0)
                put_fields(track, group, at, fields)
                cut = window_of(zero, rest, group, slot)
                fields = [times(a, b) for a, b in zip(fields, cut)]
                put_fields(
                    handed, group, 0, two_sided_each(fields, step_right[...], step_left[...], False)
                )
                return inner

            return lax.fori_loop(0, top, one, carry)

        lax.fori_loop(0, groups, one_group, 0)

    @pl.when(core == 1)
    def _():
        def one_group(group, carry):
            put_fields(handed, group, 0, fields_of(arrived, group, 0))

            def one(step, inner):
                at = pl.multiple_of((top - 1 - step) * 2 * W, 2 * W)
                fields = fields_of(handed, group, 0)
                spread = two_sided_each(fields, step_right[...], step_left[...], True)
                done = (step == 0) & (meta[PLACE] == sections - 1)
                spread = [
                    tuple(jnp.where(done, kept, fresh) for kept, fresh in zip(a, b))
                    for a, b in zip(fields, spread)
                ]
                put_fields(track, group, at, spread)
                cut = window_of(zero, rest, group, top - 1 - step)
                put_fields(handed, group, 0, [times_conjugate(a, b) for a, b in zip(cut, spread)])
                return inner

            return lax.fori_loop(0, top, one, carry)

        lax.fori_loop(0, groups, one_group, 0)


def slot_of(meta, slots, turn):
    return jnp.where(meta[PLACE] % 2 == 0, slots - 1 - turn, turn)


def second_kernel(
    meta, zero, rest, track, state, step_right, step_left, main, rim, onward, pulls, total, *, turn
):
    slots = track.shape[1] // (2 * W)
    core = meta[PLACE] % 2
    top = meta[COUNT]
    groups = zero.shape[0] // GROUP
    tile = main.shape[2]
    slot = slot_of(meta, slots, turn)
    at = pl.multiple_of(slot * 2 * W, 2 * W)
    total[...] = jnp.zeros_like(total)

    @pl.when((core == 0) & (slot < top))
    def _():
        def one_group(group, carry):
            fields = fields_of(state, group, 0)
            spread = two_sided_each(fields, step_right[...], step_left[...], True)
            waves = fields_of(track, group, at)
            put_fields(pulls, group, 0, [times_conjugate(a, b) for a, b in zip(waves, spread)])
            if turn < slots - 1:
                cut = window_of(zero, rest, group, slot)
                put_fields(onward, group, 0, [times_conjugate(a, b) for a, b in zip(cut, spread)])
            return carry

        lax.fori_loop(0, groups, one_group, 0)

    if turn < slots - 1:

        @pl.when((core == 0) & (slot >= top))
        def _():
            onward[...] = state[...]

    @pl.when((core == 1) & (slot < top))
    def _():
        def one_group(group, carry):
            fields = fields_of(state, group, 0)
            spread = fields_of(track, group, at)
            put_fields(pulls, group, 0, [times_conjugate(a, b) for a, b in zip(fields, spread)])
            if turn < slots - 1:

                @pl.when(slot < top - 1)
                def _():
                    cut = window_of(zero, rest, group, slot)
                    moving = [times(a, b) for a, b in zip(fields, cut)]
                    moving = two_sided_each(moving, step_right[...], step_left[...], False)
                    put_fields(onward, group, 0, moving)

            return carry

        lax.fori_loop(0, groups, one_group, 0)

    @pl.when(slot < top)
    def _():
        lane = lax.broadcasted_iota(jnp.int32, (W + 8, W), 1)
        spare = jnp.zeros((8, W), f32)

        def one_position(p, carry):
            row, drop, start, after, shift = at_window(meta, p, tile)
            for part in range(2):
                pull = jnp.concatenate([pulls[p, part * W : part * W + W, :], spare], 0)
                pull = pltpu.roll(pltpu.roll(pull, drop, 0), shift % W, 1)
                total[part, pl.ds(row, W + 8), pl.ds(start, W)] += jnp.where(lane >= shift, pull, 0.0)
                total[part, pl.ds(row, W + 8), pl.ds(after, W)] += jnp.where(lane < shift, pull, 0.0)
            return carry

        lax.fori_loop(0, pulls.shape[0], one_position, 0)

    main[...] = total[:, :, :tile]
    rim[...] = total[:, :, tile:]


def merge_kernel(meta, arrived, *refs):
    slots = (len(refs) - 2) // 2
    out, losses = refs[2 * slots :]
    positions = arrived.shape[0]
    for turn in range(slots):
        main, rim = refs[turn], refs[slots + turn]
        slot = slot_of(meta, slots, turn)
        out[slot, :, :, W:] = main[:, :, W:]
        out[slot, :, :, :W] = main[:, :, :W] + rim[...]
    place = lax.broadcasted_iota(jnp.int32, (1, W), 1)
    line = jnp.zeros((1, W), f32)
    for j in range(positions):
        line = jnp.where(place == j, arrived[meta[ORDER + j], 2 * W : 2 * W + 1, :], line)
    losses[...] = line[:, :positions]


VMEM = pl.BlockSpec(memory_space=pltpu.VMEM)
SMEM = pl.BlockSpec(memory_space=pltpu.SMEM)


def shards(slices, section_counts, scan_rows, scan_columns, tick_order, measured, illumination):
    slots = slices.shape[0]
    tile = slices.shape[3]
    positions = scan_rows.shape[0]
    planes = 2 * slots
    chips = lax.axis_size("depth") // 2
    place = lax.axis_index("depth")
    groups = [[2 * chip + core for chip in range(chips)] for core in range(2)]
    exchange = functools.partial(
        lax.all_to_all, axis_name="depth", split_axis=0, concat_axis=0, tiled=True, axis_index_groups=groups
    )
    params = pltpu.CompilerParams(vmem_limit_bytes=24 << 20)
    tables = [jnp.asarray(table) for table in make_tables(W)]
    meta = jnp.concatenate(
        [scan_rows, scan_columns, tick_order[0], section_counts, place.reshape(1)]
    ).astype(jnp.int32)

    def cut(base, count, rim):
        return pl.pallas_call(
            functools.partial(cut_kernel, base=base),
            out_shape=jax.ShapeDtypeStruct(
                (positions, 2 * count * W + (8 if base == 0 else 0), W), f32
            ),
            in_specs=[SMEM] + [VMEM] * 2,
            out_specs=VMEM,
            scratch_shapes=[pltpu.VMEM((2 * count, tile, tile + W), f32)],
            compiler_params=params,
            name="cut",
        )(meta, slices[:1] if base == 0 else slices, rim)

    rim_zero = moved(slices[:1, ..., :W], "lat", -1)
    zero = cut(0, 1, rim_zero)
    edge, zero = lax.optimization_barrier((slices[1:, ..., :W], zero))
    rim_rest = moved(edge, "lat", -1)
    mine_zero = exchange(zero)
    other_zero = swapped(mine_zero)
    rest = cut(1, slots - 1, rim_rest)
    sent, _ = lax.optimization_barrier((rest, mine_zero))
    mine_rest = exchange(sent)
    other_rest = swapped(mine_rest)
    boundary = pl.pallas_call(
        wave_kernel,
        out_shape=jax.ShapeDtypeStruct((chips, 2 * W + 8, W), f32),
        in_specs=[SMEM] + [VMEM] * 10,
        out_specs=VMEM,
        scratch_shapes=[pltpu.SMEM((2 * chips,), jnp.int32)],
        compiler_params=params,
        name="wave",
    )(meta, mine_zero, other_zero, mine_rest, other_rest, measured, illumination, *tables)
    arrived = exchange(boundary)
    track, handed = pl.pallas_call(
        first_kernel,
        out_shape=(
            jax.ShapeDtypeStruct((positions, planes * W, W), f32),
            jax.ShapeDtypeStruct((positions, 2 * W, W), f32),
        ),
        in_specs=[SMEM] + [VMEM] * 5,
        out_specs=(VMEM,) * 2,
        compiler_params=params,
        name="first",
    )(meta, zero, rest, arrived, *tables[:2])
    state = swapped(handed)
    mains, rims = [], []
    for turn in range(slots):
        call = pl.pallas_call(
            functools.partial(second_kernel, turn=turn),
            out_shape=(
                jax.ShapeDtypeStruct((2, tile, tile), f32),
                jax.ShapeDtypeStruct((2, tile, W), f32),
                jax.ShapeDtypeStruct((positions, 2 * W, W), f32),
            ),
            in_specs=[SMEM] + [VMEM] * 6,
            out_specs=(VMEM,) * 3,
            scratch_shapes=[
                pltpu.VMEM((positions, 2 * W, W), f32),
                pltpu.VMEM((2, tile, tile + W), f32),
            ],
            compiler_params=params,
            name="second",
        )
        main, overflow, state = call(meta, zero, rest, track, state, *tables[:2])
        rims.append(moved(overflow, "lat", 1))
        mains.append(main)
    slice_grad, losses = pl.pallas_call(
        merge_kernel,
        out_shape=(
            jax.ShapeDtypeStruct((slots, 2, tile, tile), f32),
            jax.ShapeDtypeStruct((1, positions), f32),
        ),
        in_specs=[SMEM] + [VMEM] * (1 + 2 * slots),
        out_specs=(VMEM,) * 2,
        compiler_params=params,
        name="merge",
    )(meta, arrived, *mains, *rims)
    return slice_grad, losses


def solution(mesh):
    placed = (
        P("depth", None, None, "lat"),
        P("depth"),
        P("lat"),
        P("lat"),
        P("lat", None),
        P("lat", None, None),
        P(),
    )
    return jax.shard_map(
        shards,
        mesh=mesh,
        in_specs=placed,
        out_specs=(P("depth", None, None, "lat"), P("lat", None)),
        check_vma=False,
    )
```
